256 devices in a mesh: row: 16 (over x_hi, z), col: 16 (over y, x_lo, core).
Axes of the slice: x: 4 (x_hi: 2, x_lo: 2; x = x_hi * 2 + x_lo), y: 4, z: 8, core: 2. Of those that a mesh axis runs over, the one named last changes fastest.
Arguments:
- signal: float32 [8192, 16384], P('row', 'col'), may hold values from -6 to 6
- apod: float32 [8192], P('row'), may hold values from 0.3 to 1
- coef: float32 [4, 16384], P(None, 'col'), may hold values from -0.5 to 1
- block_offset: int32 [512], P('col'), may hold values from -16 to 9
- fine_start: int32 [16384], P('col'), may hold values from 0 to 3
Outputs:
- calibrated: float32 [2, 8192, 16384], P(None, 'row', 'col')
The draws below stay inside these ranges and needn't reach their ends.
All inputs are finite; a program needn't handle non-finite values.
Results may differ from the reference program's by a relative error of at most 0.000084.
Values sent between devices are 32-bit elements; how exact they have to be, the bound alone decides.
A program may use at most 128 MiB of HBM per device.

```python
import math
import jax
import jax.numpy as jnp

TLOC = 512
TAPS = 4
HALO = 16
CB = 32
T1 = 8192
COLS = 16384
NBLK = 512
N_ROW = 16


def with_ends(values, stream_key, least, largest):
    extent = values.shape
    index_at = [jax.random.randint(jax.random.fold_in(stream_key, axis), (), 0, extent[axis]) for axis in range(len(extent))]
    values = values.at[tuple(index_at)].set(least)
    longest = extent.index(max(extent))
    index_at[longest] = (index_at[longest] + 1) % extent[longest]
    return values.at[tuple(index_at)].set(largest)


def block_levels(own_key, extent, split, smallest, high):
    def one(dim, shards_of):
        heights = jax.random.uniform(jax.random.fold_in(jax.random.fold_in(own_key, 6), dim), (shards_of,), jnp.float32, smallest / len(split), high / len(split))
        return jnp.repeat(jnp.exp(heights), extent[dim] // shards_of).reshape((-1,) + (1,) * (len(extent) - dim - 1))

    loudness = one(*split[0])
    for cut in split[1:]:
        loudness = loudness * one(*cut)
    return loudness


def gaussian(own_key, dims, scale, limit, split=(), kind=jnp.bfloat16):
    entries = jax.random.normal(own_key, dims, jnp.float32) * scale
    if len(split) > 0:
        entries = block_levels(own_key, dims, split, -0.22, 0.18) * entries
    return jnp.clip(entries, min=-limit, max=limit).astype(kind)


def setup_inputs(seed: int = 0) -> dict:
    splits = jax.random.split(jax.random.key(seed), 6)
    signal = gaussian(splits[0], (T1, COLS), 1.0, 6.0, ((0, 16), (1, 16)), jnp.float32)
    apod = jnp.clip(0.3 + 0.7 * jax.random.uniform(splits[1], (T1,), jnp.float32) ** block_levels(splits[1], (T1,), ((0, 16),), -0.2, 0.2), 0.3, 1.0)
    coef = jnp.clip(-0.5 + 1.5 * jax.random.uniform(splits[2], (TAPS, COLS), jnp.float32) ** block_levels(splits[2], (TAPS, COLS), ((1, 16),), -0.2, 0.2), -0.5, 1.0)
    block_offset = with_ends(jax.random.randint(splits[3], (NBLK,), 0 - HALO, HALO - 2 * TAPS + 2), jax.random.fold_in(splits[3], 1), 0 - HALO, (HALO - 2 * TAPS + 2) - 1).astype(jnp.int32)
    fine_start = with_ends(jax.random.randint(splits[4], (COLS,), 0, TAPS), jax.random.fold_in(splits[4], 1), 0, TAPS - 1).astype(jnp.int32)
    return {"signal": signal, "apod": apod, "coef": coef, "block_offset": block_offset, "fine_start": fine_start}


def digits_reversed(values, levels):
    result = jnp.zeros_like(values)
    for digit in range(levels):
        result = result + ((values >> digit & 1) << levels - 1 - digit)
    return result

def stencil(field, coef, first):
    padded = jnp.pad(field, ((0, 0), (HALO, HALO)))
    total = jnp.zeros_like(field)
    for tap in range(TAPS):
        total = total + coef[tap][None, :] * jnp.take(padded, first + tap, axis=1)
    return total

def reference(signal, apod, coef, block_offset, fine_start):
    apodized = signal * apod[:, None]
    spectrum = jnp.fft.fft(apodized, axis=0) / math.sqrt(T1)
    levels = N_ROW.bit_length() - 1
    rowids = jnp.arange(T1, dtype=jnp.int32)
    freq = digits_reversed(rowids // TLOC, levels) + N_ROW * (rowids % TLOC)
    spectrum = jnp.take(spectrum, freq.astype(jnp.int32), axis=0)
    colids = jnp.arange(COLS, dtype=jnp.int32)
    first = colids + jnp.repeat(block_offset, CB) + fine_start + HALO
    real_part = stencil(jnp.real(spectrum).astype(signal.dtype), coef, first.astype(jnp.int32))
    imag_part = stencil(jnp.imag(spectrum).astype(signal.dtype), coef, first.astype(jnp.int32))
    return jnp.stack([real_part, imag_part])
```

```python
import functools
import math

import jax
import jax.numpy as jnp
from jax import lax
from jax.experimental import pallas as pl
from jax.experimental.pallas import tpu as pltpu
from jax.sharding import PartitionSpec as P

MESH = pl.DeviceIdType.MESH
TAPS = 4
NZ = 8
NB = 8
LANES = 128
ROWS = 512
SLAB = ROWS // NZ
WIDE = NB * LANES
T1 = 8192
F32, BF16 = jnp.float32, jnp.bfloat16

BASE = ((0, 4, 6, 2), (1, 9, 5, 13))
PAIR_OF = ((0, 0, 1, 1, 3, 2, 2, 3), (0, 1, 2, 3, 3, 2, 1, 0))


def centre_weight(parity, plane, source):
    residue = BASE[parity][plane // 2]
    if residue == 0:
        residue = 8 * (plane % 2)
        return math.cos(2 * math.pi * (residue * source % 16) / 16)
    angle = 2 * math.pi * (residue * source % 16) / 16
    return -math.sin(angle) if plane % 2 else math.cos(angle)


def packed_pairs(parity):
    return sum(pair << 2 * z for z, pair in enumerate(PAIR_OF[parity]))


def halves(value):
    high = value.astype(BF16)
    return high, (value - high.astype(F32)).astype(BF16)


def kernel(
    x_hbm, apod_ref, coef_ref, off_ref, cos_ref, sin_ref, p_ref, q_ref, out_hbm,
    xe, xh, xl, wide_apod, field, mine, other, planes, spectra, dft_h, dft_l, y_h, y_l, result,
    load_sem, halo_send, halo_recv, own_sem, in_send, in_recv, x_send, x_recv, keep_sem, out_send, out_recv, write_sem,
):
    row, col = lax.axis_index("row"), lax.axis_index("col")
    x_hi, z = row // NZ, row % NZ
    cols = lax.axis_size("col")

    def peer(step):
        return (x_hi * NZ + (z + step) % NZ, col)

    partner = ((1 - x_hi) * NZ + z, col)
    barrier = pltpu.get_barrier_semaphore()
    for step in range(1, NZ):
        pl.semaphore_signal(barrier, inc=1, device_id=peer(step), device_id_type=MESH)
    pl.semaphore_signal(barrier, inc=1, device_id=partner, device_id_type=MESH)

    up, down = (row, (col + 1) % cols), (row, (col + cols - 1) % cols)
    for side in (up, down):
        pl.semaphore_signal(barrier, inc=1, device_id=side, device_id_type=MESH)

    load = pltpu.make_async_copy(x_hbm, xe.at[:, pl.ds(LANES, WIDE)], load_sem)
    load.start()

    for g in range(ROWS // LANES):
        line = jnp.broadcast_to(apod_ref[g : g + 1, :], (LANES, LANES))
        wide_apod[g * LANES : (g + 1) * LANES, :] = line.T

    pl.semaphore_wait(barrier, NZ + 2)

    def halo(side):
        return pltpu.make_async_remote_copy(
            src_ref=x_hbm.at[:, pl.ds((WIDE - LANES) * (1 - side), LANES)],
            dst_ref=xe.at[:, pl.ds((LANES + WIDE) * side, LANES)],
            send_sem=halo_send.at[side],
            recv_sem=halo_recv.at[side],
            device_id=(up, down)[side],
            device_id_type=MESH,
        )

    for side in range(2):
        halo(side).start()

    load.wait()

    def split_tile(t):
        at = pl.ds(t * LANES, LANES)
        high, low = halves(xe[:, at] * wide_apod[...])
        xh[:, at] = high
        xl[:, at] = low

    def stencil_block(b):
        at = pl.ds(pl.multiple_of(b * LANES, LANES), LANES)
        window = pl.ds(pl.multiple_of(b * LANES, LANES), 3 * LANES)
        shape = (3 * LANES, LANES)
        first = lax.broadcasted_iota(jnp.int32, (1, LANES), 1) + LANES + off_ref[:, at]
        tap = lax.broadcasted_iota(jnp.int32, shape, 0) - first
        band = jnp.zeros(shape, F32)
        for q in range(TAPS):
            band = jnp.where(tap == q, coef_ref[q : q + 1, at], band)
        band_h, band_l = halves(band)
        xw = xh[:, window]
        field[b] = (
            jnp.dot(xw, band_h, preferred_element_type=F32)
            + jnp.dot(xw, band_l, preferred_element_type=F32)
            + jnp.dot(xl[:, window], band_h, preferred_element_type=F32)
        )

    def send_in(b):
        pltpu.make_async_copy(
            field.at[b, pl.ds(z * SLAB, SLAB)], mine.at[b, z], own_sem.at[b]
        ).start()
        for step in (4, 3, 5, 2, 6, 1, 7):
            centre = (z + step) % NZ
            pltpu.make_async_remote_copy(
                src_ref=field.at[b, pl.ds(centre * SLAB, SLAB)],
                dst_ref=mine.at[b, z],
                send_sem=in_send.at[b],
                recv_sem=in_recv.at[b],
                device_id=peer(step),
                device_id_type=MESH,
            ).start()

    for t in range(1, NB + 1):
        split_tile(t)

    @pl.loop(2, NB - 1)
    def _(b):
        stencil_block(b)
        send_in(b)

    for side in range(2):
        halo(side).wait_recv()

    @pl.when(col == 0)
    def _():
        xe[:, :LANES] = jnp.zeros((ROWS, LANES), F32)

    @pl.when(col == cols - 1)
    def _():
        xe[:, LANES + WIDE :] = jnp.zeros((ROWS, LANES), F32)

    split_tile(0)
    split_tile(NB + 1)

    @pl.loop(NB - 1, NB + 2)
    def _(i):
        b = i % NB
        stencil_block(b)
        send_in(b)

    @pl.loop(0, 32)
    def _(k):
        c, s = cos_ref[pl.ds(k, 1), :], sin_ref[pl.ds(k, 1), :]
        p, q = p_ref[...], q_ref[...]
        top = halves(c * p - s * q)
        low = halves(-(s * p + c * q))
        for at, (high, rest) in ((0, top), (ROWS, low)):
            rows = pl.ds(pl.multiple_of(at + k * 16, 16), 16)
            dft_h[rows, :] = high
            dft_l[rows, :] = rest

    def exchange(b):
        return pltpu.make_async_remote_copy(
            src_ref=mine.at[b],
            dst_ref=other.at[b],
            send_sem=x_send.at[b],
            recv_sem=x_recv.at[b],
            device_id=partner,
            device_id_type=MESH,
        )

    def pass_on(b):
        pltpu.make_async_copy(field.at[b, pl.ds(0, SLAB)], mine.at[b, z], own_sem.at[b]).wait()
        pltpu.make_async_copy(
            mine.at[b, pl.ds(0, NZ - 1)], mine.at[b, pl.ds(0, NZ - 1)], in_recv.at[b]
        ).wait()
        exchange(b).start()

    sign = (1 - 2 * x_hi).astype(F32)
    weights = [
        [
            jnp.where(x_hi == 0, centre_weight(0, o, s), centre_weight(1, o, s)).astype(F32)
            for s in range(NZ)
        ]
        for o in range(NZ)
    ]
    pairs = packed_pairs(0) + x_hi * (packed_pairs(1) - packed_pairs(0))

    def pair_of(place):
        return lax.shift_right_logical(pairs, 2 * place) & 3

    def centre_of(b):
        exchange(b).wait_recv()
        step = 16
        for part in range(SLAB // step):
            at = pl.ds(part * step, step)
            terms = [other[b, s, at] + sign * mine[b, s, at] for s in range(NZ)]
            for o in range(NZ):
                total = weights[o][0] * terms[0]
                for s in range(1, NZ):
                    total = total + weights[o][s] * terms[s]
                planes[b, o // 2, pl.ds(SLAB * (o % 2) + part * step, step)] = total

    def slot(b):
        return spectra.at[
            b // 2,
            pl.ds(pl.multiple_of(z * LANES, LANES), LANES),
            pl.ds(pl.multiple_of(b % 2 * LANES, LANES), LANES),
        ]

    def send_out(b):
        pltpu.make_async_copy(planes.at[b, pair_of(z)], slot(b), keep_sem.at[b]).start()
        for step in (4, 3, 5, 2, 6, 1, 7):
            pltpu.make_async_remote_copy(
                src_ref=planes.at[b, pair_of((z + step) % NZ)],
                dst_ref=slot(b),
                send_sem=out_send.at[b],
                recv_sem=out_recv.at[b],
                device_id=peer(step),
                device_id_type=MESH,
            ).start()

    pass_on(2)

    @pl.loop(3, NB + 2)
    def _(i):
        pass_on(i % NB)
        b = (i - 1) % NB
        centre_of(b)
        send_out(b)

    centre_of(1)
    send_out(1)

    def write(c):
        return pltpu.make_async_copy(
            result.at[c], out_hbm.at[:, :, pl.ds(pl.multiple_of(c * 256, 256), 256)], write_sem.at[c]
        )

    @pl.loop(1, 5)
    def _(i):
        c = i % 4
        for b in (2 * c, 2 * c + 1):
            pltpu.make_async_copy(planes.at[b, 0], slot(b), keep_sem.at[b]).wait()
            pltpu.make_async_copy(
                spectra.at[c, pl.ds(0, 7 * LANES), pl.ds(0, LANES)],
                spectra.at[c, pl.ds(0, 7 * LANES), pl.ds(0, LANES)],
                out_recv.at[b],
            ).wait()
        high, low = halves(spectra[c])
        y_h[...] = high
        y_l[...] = low
        for part in range(4):
            rows = pl.ds(part * 256, 256)
            result[c, part // 2, pl.ds(part % 2 * 256, 256)] = (
                jnp.dot(dft_h[rows, :], y_h[...], preferred_element_type=F32)
                + jnp.dot(dft_h[rows, :], y_l[...], preferred_element_type=F32)
                + jnp.dot(dft_l[rows, :], y_h[...], preferred_element_type=F32)
            )
        write(c).start()

    for side in range(2):
        halo(side).wait_send()

    @pl.loop(0, NB)
    def _(b):
        seven = mine.at[b, pl.ds(0, NZ - 1)]
        pltpu.make_async_copy(seven, seven, in_send.at[b]).wait()
        exchange(b).wait_send()
        sent = spectra.at[b // 2, pl.ds(0, 7 * LANES), pl.ds(0, LANES)]
        pltpu.make_async_copy(sent, sent, out_send.at[b]).wait()

    for c in range(4):
        write(c).wait()


def tables(x_hi, z):
    lane = jnp.arange(WIDE, dtype=jnp.int32)
    time = SLAB * (lane // LANES) + lane % SLAB
    plane = lane % LANES // SLAB
    residue = 8 * (z % 2) + 4 * (z // 2 % 2) + 2 * (z // 4) + x_hi
    step = jnp.arange(32, dtype=jnp.int32)[:, None]
    turn = 2.0 * math.pi / T1
    coarse = turn * (256 * step * time[None, :] % T1).astype(F32)
    alone = residue % 8 == 0
    quarter = jnp.where((plane == 1) & ~alone, 3 * T1 // 4, 0)
    base = jnp.where(x_hi == 0, residue < 8, residue % 4 == 1)
    size = jnp.where(
        alone,
        jnp.where(plane == residue // 8, 1.0, 0.0),
        jnp.where((plane == 1) & ~base, -1.0, 1.0),
    ) / math.sqrt(T1)
    fine = turn * ((time[None, :] * (16 * step[:16] + residue) + quarter[None, :]) % T1).astype(F32)
    return jnp.cos(coarse), jnp.sin(coarse), size * jnp.cos(fine), size * jnp.sin(fine)


def on_device(signal, apod, coef, block_offset, fine_start):
    row = lax.axis_index("row")
    off = (jnp.repeat(block_offset, WIDE // block_offset.shape[0]) + fine_start)[None, :]
    cosine, sine, p, q = tables(row // NZ, row % NZ)
    vmem, anywhere = (pl.BlockSpec(memory_space=pltpu.VMEM), pl.BlockSpec(memory_space=pl.ANY))
    sem = pltpu.SemaphoreType.DMA
    return pl.pallas_call(
        kernel,
        name="f1_section",
        out_shape=jax.ShapeDtypeStruct((2, ROWS, WIDE), F32),
        in_specs=[anywhere] + [vmem] * 7,
        out_specs=anywhere,
        scratch_shapes=[
            pltpu.VMEM((ROWS, WIDE + 2 * LANES), F32),
            pltpu.VMEM((ROWS, WIDE + 2 * LANES), BF16),
            pltpu.VMEM((ROWS, WIDE + 2 * LANES), BF16),
            pltpu.VMEM((ROWS, LANES), F32),
            pltpu.VMEM((NB, ROWS, LANES), F32),
            pltpu.VMEM((NB, NZ, SLAB, LANES), F32),
            pltpu.VMEM((NB, NZ, SLAB, LANES), F32),
            pltpu.VMEM((NB, 4, LANES, LANES), F32),
            pltpu.VMEM((NB // 2, WIDE, 2 * LANES), F32),
            pltpu.VMEM((WIDE, WIDE), BF16),
            pltpu.VMEM((WIDE, WIDE), BF16),
            pltpu.VMEM((WIDE, 2 * LANES), BF16),
            pltpu.VMEM((WIDE, 2 * LANES), BF16),
            pltpu.VMEM((NB // 2, 2, ROWS, 2 * LANES), F32),
            sem,
            sem((2,)),
            sem((2,)),
            sem((NB,)),
            sem((NB,)),
            sem((NB,)),
            sem((NB,)),
            sem((NB,)),
            sem((NB,)),
            sem((NB,)),
            sem((NB,)),
            sem((4,)),
        ],
        compiler_params=pltpu.CompilerParams(
            collective_id=0, has_side_effects=True, vmem_limit_bytes=56 << 20
        ),
    )(signal, apod.reshape(ROWS // LANES, LANES), coef, off, cosine, sine, p, q)


def solution(mesh):
    placed = (P("row", "col"), P("row"), P(None, "col"), P("col"), P("col"))
    return jax.shard_map(
        on_device, mesh=mesh, in_specs=placed, out_specs=P(None, "row", "col"), check_vma=False
    )
```

```python
import functools
import math

import jax
import jax.numpy as jnp
import numpy as np
from jax import lax
from jax.experimental import pallas as pl
from jax.experimental.pallas import tpu as pltpu
from jax.sharding import PartitionSpec as P

MESH = pl.DeviceIdType.MESH
TAPS = 4
NZ = 8
NB = 8
LANES = 128
ROWS = 512
SLAB = ROWS // NZ
WIDE = NB * LANES
T1 = 8192
F32, BF16 = jnp.float32, jnp.bfloat16


def residue_of(row):
    digits = row % 2 * 8 + row // 2 % 2 * 4 + row // 4 % 2 * 2 + row // 8
    return digits


NEAR = (-2, -1, 0, 1)
HOPS = 5
START = (None, 0, 5, 9, 12, 14)
TRAVELLING = 15
KEPT = tuple((slab, 0) for slab in NEAR)
SENT = ((-2, 2), (1, -2), (-2, 1), (1, -1))


def sources(slab):
    return [0] + [-hop for hop in range(1, 4 - slab)] + [hop for hop in range(1, 5 + slab)]


def centre_weights():
    table = np.zeros((16, NZ, 2, NZ))
    for row in range(16):
        x_hi, z = divmod(row, NZ)
        for i, (slab, owner) in enumerate(KEPT + SENT):
            residue = residue_of(x_hi * NZ + (z + owner) % NZ)
            for j, source in enumerate(sources(slab)):
                turn = residue * ((z + source) % NZ) % 16
                table[row, i, 0, j] = np.cos(turn * np.pi / 8)
                table[row, i, 1, j] = -np.sin(turn * np.pi / 8) if turn % 8 else 0.0
    return table.reshape(-1).astype(np.float32)


def transform_tables():
    lane = np.arange(WIDE)
    time = SLAB * (lane // LANES) + lane % SLAB
    plane = lane % LANES // SLAB
    coarse = 256 * np.arange(32)[:, None] * time
    fine = 16 * np.arange(16)[:, None] * time
    own = np.array([residue_of(row) for row in range(16)])[:, None] * time - T1 // 4 * plane
    parts = []
    for steps, size in ((coarse, 1.0), (fine, 1.0), (own, 1.0 / math.sqrt(T1))):
        angle = 2.0 * np.pi / T1 * (steps % T1)
        parts += [size * np.cos(angle), size * np.sin(angle)]
    return np.concatenate(parts).astype(np.float32)


def halves(value):
    high = value.astype(BF16)
    return high, (value - high.astype(F32)).astype(BF16)


def kernel(
    weight_ref, block_ref, x_hbm, table_hbm, apod_ref, coef_ref, fine_ref, out_hbm,
    xe, xh, xl, wide_apod, field, other, even, risen, sunk, planes, spectra, table, dft_h, dft_l, y_h, y_l, result,
    load_sem, table_sem, halo_send, halo_recv, x_send, x_recv, up_send, up_recv, down_send, down_recv,
    out_send, out_recv, write_sem,
):
    row, col = lax.axis_index("row"), lax.axis_index("col")
    x_hi, z = row // NZ, row % NZ
    cols = lax.axis_size("col")

    def peer(step):
        return (x_hi * NZ + (z + step + NZ) % NZ, col)

    partner = ((1 - x_hi) * NZ + z, col)
    up, down = (row, (col + 1) % cols), (row, (col + cols - 1) % cols)
    barrier = pltpu.get_barrier_semaphore()
    greeted = [peer(step) for step in (1, 2, -1, -2)] + [partner, up, down]
    for device in greeted:
        pl.semaphore_signal(barrier, inc=1, device_id=device, device_id_type=MESH)

    def load(t):
        return pltpu.make_async_copy(
            x_hbm.at[:, pl.ds((t - 1) * LANES, LANES)], xe.at[:, pl.ds(t * LANES, LANES)], load_sem.at[t]
        )

    for t in (2, 3, 4, 5, 6, 7, 8, 1):
        load(t).start()
    tables = pltpu.make_async_copy(table_hbm, table, table_sem)
    tables.start()

    for g in range(ROWS // LANES):
        line = jnp.broadcast_to(apod_ref[g : g + 1, :], (LANES, LANES))
        wide_apod[g * LANES : (g + 1) * LANES, :] = line.T

    def split_tile(t):
        at = pl.ds(t * LANES, LANES)
        high, low = halves(xe[:, at] * wide_apod[...])
        xh[:, at] = high
        xl[:, at] = low

    def stencil_block(b):
        at, window = pl.ds(b * LANES, LANES), pl.ds(b * LANES, 3 * LANES)
        shape = (3 * LANES, LANES)
        lane = lax.broadcasted_iota(jnp.int32, (1, LANES), 1)
        first = lane + LANES + fine_ref[b : b + 1, :]
        for part in range(4):
            inside = lane // 32 == part
            first = first + jnp.where(inside, block_ref[4 * b + part], 0)
        tap = lax.broadcasted_iota(jnp.int32, shape, 0) - first
        band = jnp.zeros(shape, F32)
        for q in range(TAPS):
            band = jnp.where(tap == q, coef_ref[q : q + 1, at], band)
        band_h, band_l = halves(band)
        xw = xh[:, window]
        field[b] = (
            jnp.dot(xw, band_h, preferred_element_type=F32)
            + jnp.dot(xw, band_l, preferred_element_type=F32)
            + jnp.dot(xl[:, window], band_h, preferred_element_type=F32)
        )

    def exchange(b):
        return pltpu.make_async_remote_copy(
            src_ref=field.at[b],
            dst_ref=other.at[b],
            send_sem=x_send.at[b],
            recv_sem=x_recv.at[b],
            device_id=partner,
            device_id_type=MESH,
        )

    def halo(side):
        return pltpu.make_async_remote_copy(
            src_ref=x_hbm.at[:, pl.ds((WIDE - LANES) * (1 - side), LANES)],
            dst_ref=xe.at[:, pl.ds((LANES + WIDE) * side, LANES)],
            send_sem=halo_send.at[side],
            recv_sem=halo_recv.at[side],
            device_id=(up, down)[side],
            device_id_type=MESH,
        )

    for t in (2, 3):
        load(t).wait()
        split_tile(t)
    for b in range(2, 7):
        load(b + 2).wait()
        split_tile(b + 2)
        stencil_block(b)
        if b == 2:
            pl.semaphore_wait(barrier, len(greeted))
            for side in range(2):
                halo(side).start()
        exchange(b).start()
    load(1).wait()
    split_tile(1)
    stencil_block(1)
    exchange(1).start()

    for side in range(2):
        halo(side).wait_recv()

    @pl.when(col == 0)
    def _():
        xe[:, :LANES] = jnp.zeros((ROWS, LANES), F32)

    @pl.when(col == cols - 1)
    def _():
        xe[:, LANES + WIDE :] = jnp.zeros((ROWS, LANES), F32)

    split_tile(NB + 1)
    stencil_block(7)
    exchange(7).start()
    split_tile(0)
    stencil_block(0)
    exchange(0).start()

    tables.wait()
    own_c, own_s = table[pl.ds(96 + row, 1), :], table[pl.ds(112 + row, 1), :]
    p = table[64:80, :] * own_c - table[80:96, :] * own_s
    q = table[80:96, :] * own_c + table[64:80, :] * own_s
    table[64:80, :] = p
    table[80:96, :] = q

    @pl.loop(0, 32)
    def _(k):
        c, s = table[pl.ds(k, 1), :], table[pl.ds(32 + k, 1), :]
        p, q = table[64:80, :], table[80:96, :]
        top = halves(c * p - s * q)
        low = halves(-(s * p + c * q))
        for at, (high, rest) in ((0, top), (ROWS, low)):
            rows = pl.ds(pl.multiple_of(at + k * 16, 16), 16)
            for i in range(NZ):
                lanes = pl.ds(pl.multiple_of((i - z + 2 + NZ) % NZ * LANES, LANES), LANES)
                dft_h[rows, lanes] = high[:, i * LANES : (i + 1) * LANES]
                dft_l[rows, lanes] = rest[:, i * LANES : (i + 1) * LANES]

    def arrived(ref, sem):
        pltpu.make_async_copy(ref, ref, sem).wait()

    def rise(b, hop):
        if hop == 1:
            source = even.at[b, pl.ds(3, 5)]
        else:
            source = risen.at[b, pl.ds(START[hop - 1] + 1, 6 - hop)]
        return pltpu.make_async_remote_copy(
            src_ref=source,
            dst_ref=risen.at[b, pl.ds(START[hop], 6 - hop)],
            send_sem=up_send.at[b, hop - 1],
            recv_sem=up_recv.at[b, hop - 1],
            device_id=peer(1),
            device_id_type=MESH,
        )

    def sink(b, hop):
        if hop == 1:
            source = even.at[b, pl.ds(0, 5)]
        else:
            source = sunk.at[b, pl.ds(START[hop - 1], 6 - hop)]
        return pltpu.make_async_remote_copy(
            src_ref=source,
            dst_ref=sunk.at[b, pl.ds(START[hop], 6 - hop)],
            send_sem=down_send.at[b, hop - 1],
            recv_sem=down_recv.at[b, hop - 1],
            device_id=peer(-1),
            device_id_type=MESH,
        )

    sign = (1 - 2 * x_hi).astype(F32)

    def depart(b):
        exchange(b).wait_recv()
        for i in range(NZ):
            rows = pl.ds(pl.multiple_of((z + i + 4) % NZ * SLAB, SLAB), SLAB)
            even[b, i] = other[b, rows] + sign * field[b, rows]
        rise(b, 1).start()
        sink(b, 1).start()

    def relay(b, hop):
        rise(b, hop - 1).wait_recv()
        rise(b, hop).start()
        sink(b, hop - 1).wait_recv()
        sink(b, hop).start()

    def terms_of(b, slab, rows):
        terms = [even[b, slab + 4, rows]]
        terms += [risen[b, START[hop] + slab + 2, rows] for hop in range(1, 4 - slab)]
        terms += [sunk[b, START[hop] + slab + 4 - hop, rows] for hop in range(1, 5 + slab)]
        return terms

    def centre_of(b):
        rise(b, HOPS).wait_recv()
        sink(b, HOPS).wait_recv()
        step = 16
        lanes = pl.ds(pl.multiple_of(b % 2 * LANES, LANES), LANES)

        @pl.loop(0, SLAB // step)
        def _(part):
            at = pl.multiple_of(part * step, step)
            for slab in NEAR:
                terms = terms_of(b, slab, pl.ds(at, step))
                for i, (which, owner) in enumerate(KEPT + SENT):
                    if which != slab:
                        continue
                    for plane in range(2):
                        base = ((row * NZ + i) * 2 + plane) * NZ
                        total = weight_ref[base] * terms[0]
                        for j in range(1, NZ):
                            total = total + weight_ref[base + j] * terms[j]
                        if owner == 0:
                            rows = pl.ds((slab + 2) * LANES + SLAB * plane + at, step)
                            spectra[b // 2, rows, lanes] = total
                        else:
                            planes[b, i - len(KEPT), pl.ds(SLAB * plane + at, step)] = total

    def send_out(b):
        for i, (slab, owner) in enumerate(SENT):
            pltpu.make_async_remote_copy(
                src_ref=planes.at[b, i],
                dst_ref=spectra.at[
                    b // 2,
                    pl.ds((slab - owner + 2) % NZ * LANES, LANES),
                    pl.ds(pl.multiple_of(b % 2 * LANES, LANES), LANES),
                ],
                send_sem=out_send.at[b],
                recv_sem=out_recv.at[b],
                device_id=peer(owner),
                device_id_type=MESH,
            ).start()

    def nth(i):
        return jnp.where(i < 5, i + 2, jnp.where(i == 5, 1, 7 * (7 - i)))

    def write(c):
        return pltpu.make_async_copy(
            result.at[c], out_hbm.at[:, :, pl.ds(pl.multiple_of(c * 256, 256), 256)], write_sem.at[c]
        )

    def product(c, near):
        half = pl.ds(0 if near else WIDE // 2, WIDE // 2)
        high, low = halves(spectra[c, half, :])
        y_h[half, :] = high
        y_l[half, :] = low
        for part in range(4):
            rows = pl.ds(part * 256, 256)
            total = (
                jnp.dot(dft_h[rows, half], y_h[half, :], preferred_element_type=F32)
                + jnp.dot(dft_h[rows, half], y_l[half, :], preferred_element_type=F32)
                + jnp.dot(dft_l[rows, half], y_h[half, :], preferred_element_type=F32)
            )
            to = (c, part // 2, pl.ds(part % 2 * 256, 256))
            result[to] = total if near else result[to] + total

    def chunk(i):
        c = jnp.where(i < 2, i + 1, 3 * (3 - i))
        product(c, True)
        for b in (2 * c, 2 * c + 1):
            arrived(planes.at[b], out_recv.at[b])
        product(c, False)
        write(c).start()

    @pl.loop(0, NB + HOPS + 1)
    def _(i):
        for hop in range(HOPS, 1, -1):
            at = i - hop + 1

            @pl.when((at >= 0) & (at < NB))
            def _(at=at, hop=hop):
                relay(nth(at), hop)

        @pl.when(i < NB)
        def _():
            depart(nth(i))

        at = i - HOPS

        @pl.when((at >= 0) & (at < NB))
        def _():
            b = nth(at)
            centre_of(b)
            send_out(b)

        late = i - HOPS - 2

        @pl.when((late > 0) & (late % 2 == 1))
        def _():
            chunk(late // 2)

    chunk(3)

    for side in range(2):
        halo(side).wait_send()

    @pl.loop(0, NB)
    def _(b):
        exchange(b).wait_send()
        for hop in range(1, HOPS + 1):
            rise(b, hop).wait_send()
            sink(b, hop).wait_send()
        arrived(planes.at[b], out_send.at[b])

    for c in range(4):
        write(c).wait()


def on_device(signal, apod, coef, block_offset, fine_start):
    vmem, smem = (pl.BlockSpec(memory_space=pltpu.VMEM), pl.BlockSpec(memory_space=pltpu.SMEM))
    anywhere = pl.BlockSpec(memory_space=pl.ANY)
    sem = pltpu.SemaphoreType.DMA
    extended = WIDE + 2 * LANES
    return pl.pallas_call(
        kernel,
        name="f1_section",
        out_shape=jax.ShapeDtypeStruct((2, ROWS, WIDE), F32),
        in_specs=[smem, smem, anywhere, anywhere, vmem, vmem, vmem],
        out_specs=anywhere,
        scratch_shapes=[
            pltpu.VMEM((ROWS, extended), F32),
            pltpu.VMEM((ROWS, extended), BF16),
            pltpu.VMEM((ROWS, extended), BF16),
            pltpu.VMEM((ROWS, LANES), F32),
            pltpu.VMEM((NB, ROWS, LANES), F32),
            pltpu.VMEM((NB, ROWS, LANES), F32),
            pltpu.VMEM((NB, NZ, SLAB, LANES), F32),
            pltpu.VMEM((NB, TRAVELLING, SLAB, LANES), F32),
            pltpu.VMEM((NB, TRAVELLING, SLAB, LANES), F32),
            pltpu.VMEM((NB, len(SENT), LANES, LANES), F32),
            pltpu.VMEM((NB // 2, WIDE, 2 * LANES), F32),
            pltpu.VMEM((LANES, WIDE), F32),
            pltpu.VMEM((WIDE, WIDE), BF16),
            pltpu.VMEM((WIDE, WIDE), BF16),
            pltpu.VMEM((WIDE, 2 * LANES), BF16),
            pltpu.VMEM((WIDE, 2 * LANES), BF16),
            pltpu.VMEM((NB // 2, 2, ROWS, 2 * LANES), F32),
            sem((NB + 1,)),
            sem,
            sem((2,)),
            sem((2,)),
            sem((NB,)),
            sem((NB,)),
            sem((NB, HOPS)),
            sem((NB, HOPS)),
            sem((NB, HOPS)),
            sem((NB, HOPS)),
            sem((NB,)),
            sem((NB,)),
            sem((4,)),
        ],
        compiler_params=pltpu.CompilerParams(
            collective_id=0, has_side_effects=True, vmem_limit_bytes=60 << 20
        ),
    )(
        centre_weights(),
        block_offset,
        signal,
        transform_tables(),
        apod.reshape(ROWS // LANES, LANES),
        coef,
        fine_start.reshape(NB, LANES),
    )


def solution(mesh):
    placed = (P("row", "col"), P("row"), P(None, "col"), P("col"), P("col"))
    return jax.shard_map(
        on_device, mesh=mesh, in_specs=placed, out_specs=P(None, "row", "col"), check_vma=False
    )
```

```python
import functools
import math

import jax
import jax.numpy as jnp
import numpy as np
from jax import lax
from jax.experimental import pallas as pl
from jax.experimental.pallas import tpu as pltpu
from jax.sharding import PartitionSpec as P

MESH = pl.DeviceIdType.MESH
TAPS = 4
NZ = 8
NB = 8
LANES = 128
ROWS = 512
SLAB = ROWS // NZ
WIDE = NB * LANES
T1 = 8192
F32, BF16 = jnp.float32, jnp.bfloat16


def residue_of(row):
    digits = row % 2 * 8 + row // 2 % 2 * 4 + row // 4 % 2 * 2 + row // 8
    return digits


NEAR = (-2, -1, 0, 1)
HOPS = 5
RAW = 2
START = (None, 0, 5, 9, 12, 14)
TRAVELLING = 15
KEPT = tuple((slab, 0) for slab in NEAR)
SENT = ((-2, 2), (1, -2), (-2, 1), (1, -1))


def sources(slab):
    return [0] + [-hop for hop in range(1, 4 - slab)] + [hop for hop in range(1, 5 + slab)]


def centre_weights():
    table = np.zeros((16, NZ, 2, NZ))
    for row in range(16):
        x_hi, z = divmod(row, NZ)
        for i, (slab, owner) in enumerate(KEPT + SENT):
            residue = residue_of(x_hi * NZ + (z + owner) % NZ)
            for j, source in enumerate(sources(slab)):
                turn = residue * ((z + source) % NZ) % 16
                table[row, i, 0, j] = np.cos(turn * np.pi / 8)
                table[row, i, 1, j] = -np.sin(turn * np.pi / 8) if turn % 8 else 0.0
    return table.reshape(-1).astype(np.float32)


def transform_tables():
    lane = np.arange(WIDE)
    time = SLAB * (lane // LANES) + lane % SLAB
    plane = lane % LANES // SLAB
    coarse = 256 * np.arange(32)[:, None] * time
    fine = 16 * np.arange(16)[:, None] * time
    own = np.array([residue_of(row) for row in range(16)])[:, None] * time - T1 // 4 * plane
    parts = []
    for steps, size in ((coarse, 1.0), (fine, 1.0), (own, 1.0 / math.sqrt(T1))):
        angle = 2.0 * np.pi / T1 * (steps % T1)
        parts += [size * np.cos(angle), size * np.sin(angle)]
    return np.concatenate(parts).astype(np.float32)


def halves(value):
    high = value.astype(BF16)
    return high, (value - high.astype(F32)).astype(BF16)


def kernel(
    weight_hbm, block_hbm, x_hbm, table_hbm, apod_hbm, coef_hbm, fine_hbm, result,
    weight_ref, block_ref, apod_ref, coef_ref, fine_ref, xe, xh, xl, wide_apod, field, other, even, risen, sunk,
    other_even, other_risen, other_sunk, planes, spectra, table, dft_h, dft_l, y_h, y_l,
    small_sem, load_sem, table_sem, halo_send, halo_recv, x_send, x_recv, late_send, late_recv, up_send, up_recv, down_send, down_recv,
    out_send, out_recv,
):
    row, col = lax.axis_index("row"), lax.axis_index("col")
    x_hi, z = row // NZ, row % NZ
    cols = lax.axis_size("col")

    def peer(step):
        return (x_hi * NZ + (z + step + NZ) % NZ, col)

    partner = ((1 - x_hi) * NZ + z, col)
    up, down = (row, (col + 1) % cols), (row, (col + cols - 1) % cols)
    barrier = pltpu.get_barrier_semaphore()
    greeted = [peer(step) for step in (1, 2, -1, -2)] + [partner, up, down]
    for device in greeted:
        pl.semaphore_signal(barrier, inc=1, device_id=device, device_id_type=MESH)

    def load(t):
        return pltpu.make_async_copy(
            x_hbm.at[:, pl.ds((t - 1) * LANES, LANES)], xe.at[:, pl.ds(t * LANES, LANES)], load_sem.at[t]
        )

    small = [
        pltpu.make_async_copy(source, target, small_sem.at[i])
        for i, (source, target) in enumerate(
            (
                (apod_hbm, apod_ref),
                (coef_hbm, coef_ref),
                (fine_hbm, fine_ref),
                (block_hbm, block_ref),
                (weight_hbm, weight_ref),
            )
        )
    ]
    for copy in small:
        copy.start()
    for t in (2, 3, 4, 5, 6, 7, 8, 1):
        load(t).start()
    tables = pltpu.make_async_copy(table_hbm, table, table_sem)
    tables.start()

    for copy in small:
        copy.wait()

    for g in range(ROWS // LANES):
        line = jnp.broadcast_to(apod_ref[g : g + 1, :], (LANES, LANES))
        wide_apod[g * LANES : (g + 1) * LANES, :] = line.T

    def split_tile(t):
        at = pl.ds(t * LANES, LANES)
        high, low = halves(xe[:, at] * wide_apod[...])
        xh[:, at] = high
        xl[:, at] = low

    def stencil_block(b):
        at, window = pl.ds(b * LANES, LANES), pl.ds(b * LANES, 3 * LANES)
        shape = (3 * LANES, LANES)
        lane = lax.broadcasted_iota(jnp.int32, (1, LANES), 1)
        first = lane + LANES + fine_ref[b : b + 1, :]
        for part in range(4):
            inside = lane // 32 == part
            first = first + jnp.where(inside, block_ref[4 * b + part], 0)
        tap = lax.broadcasted_iota(jnp.int32, shape, 0) - first
        band = jnp.zeros(shape, F32)
        for q in range(TAPS):
            band = jnp.where(tap == q, coef_ref[q : q + 1, at], band)
        band_h, band_l = halves(band)
        xw = xh[:, window]
        field[b] = (
            jnp.dot(xw, band_h, preferred_element_type=F32)
            + jnp.dot(xw, band_l, preferred_element_type=F32)
            + jnp.dot(xl[:, window], band_h, preferred_element_type=F32)
        )

    def exchange(b):
        return pltpu.make_async_remote_copy(
            src_ref=field.at[b],
            dst_ref=other.at[b],
            send_sem=x_send.at[b],
            recv_sem=x_recv.at[b],
            device_id=partner,
            device_id_type=MESH,
        )

    def rise(b, hop):
        if hop == 1:
            source = even.at[b, pl.ds(3, 5)]
        else:
            source = risen.at[b, pl.ds(START[hop - 1] + 1, 6 - hop)]
        return pltpu.make_async_remote_copy(
            src_ref=source,
            dst_ref=risen.at[b, pl.ds(START[hop], 6 - hop)],
            send_sem=up_send.at[b, hop - 1],
            recv_sem=up_recv.at[b, hop - 1],
            device_id=peer(1),
            device_id_type=MESH,
        )

    def sink(b, hop):
        if hop == 1:
            source = even.at[b, pl.ds(0, 5)]
        else:
            source = sunk.at[b, pl.ds(START[hop - 1], 6 - hop)]
        return pltpu.make_async_remote_copy(
            src_ref=source,
            dst_ref=sunk.at[b, pl.ds(START[hop], 6 - hop)],
            send_sem=down_send.at[b, hop - 1],
            recv_sem=down_recv.at[b, hop - 1],
            device_id=peer(-1),
            device_id_type=MESH,
        )

    def depart_raw(b):
        for i in range(NZ):
            rows = pl.ds(pl.multiple_of((z + i + 4) % NZ * SLAB, SLAB), SLAB)
            even[b, i] = field[b, rows]
        rise(b, 1).start()
        sink(b, 1).start()

    def halo(side):
        return pltpu.make_async_remote_copy(
            src_ref=x_hbm.at[:, pl.ds((WIDE - LANES) * (1 - side), LANES)],
            dst_ref=xe.at[:, pl.ds((LANES + WIDE) * side, LANES)],
            send_sem=halo_send.at[side],
            recv_sem=halo_recv.at[side],
            device_id=(up, down)[side],
            device_id_type=MESH,
        )

    for t in (2, 3):
        load(t).wait()
        split_tile(t)
    for b in range(2, 7):
        load(b + 2).wait()
        split_tile(b + 2)
        stencil_block(b)
        if b == 2:
            pl.semaphore_wait(barrier, len(greeted))
        if b < 2 + RAW:
            depart_raw(b)
        else:
            exchange(b).start()
        if b == 3:
            for side in range(2):
                halo(side).start()
    load(1).wait()
    split_tile(1)
    stencil_block(1)
    exchange(1).start()

    def outermost():
        for side in range(2):
            halo(side).wait_recv()

        @pl.when(col == 0)
        def _():
            xe[:, :LANES] = jnp.zeros((ROWS, LANES), F32)

        @pl.when(col == cols - 1)
        def _():
            xe[:, LANES + WIDE :] = jnp.zeros((ROWS, LANES), F32)

        split_tile(NB + 1)
        stencil_block(7)
        exchange(7).start()
        split_tile(0)
        stencil_block(0)
        exchange(0).start()

    def build_transform():
        tables.wait()
        own_c, own_s = table[pl.ds(96 + row, 1), :], table[pl.ds(112 + row, 1), :]
        p = table[64:80, :] * own_c - table[80:96, :] * own_s
        q = table[80:96, :] * own_c + table[64:80, :] * own_s
        table[64:80, :] = p
        table[80:96, :] = q

        @pl.loop(0, 32)
        def _(k):
            c, s = table[pl.ds(k, 1), :], table[pl.ds(32 + k, 1), :]
            p, q = table[64:80, :], table[80:96, :]
            top = halves(c * p - s * q)
            low = halves(-(s * p + c * q))
            for at, (high, rest) in ((0, top), (ROWS, low)):
                rows = pl.ds(pl.multiple_of(at + k * 16, 16), 16)
                for i in range(NZ):
                    lanes = pl.ds(pl.multiple_of((i - z + 2 + NZ) % NZ * LANES, LANES), LANES)
                    dft_h[rows, lanes] = high[:, i * LANES : (i + 1) * LANES]
                    dft_l[rows, lanes] = rest[:, i * LANES : (i + 1) * LANES]

    def arrived(ref, sem):
        pltpu.make_async_copy(ref, ref, sem).wait()

    sign = (1 - 2 * x_hi).astype(F32)

    def depart(b):
        exchange(b).wait_recv()
        for i in range(NZ):
            rows = pl.ds(pl.multiple_of((z + i + 4) % NZ * SLAB, SLAB), SLAB)
            even[b, i] = other[b, rows] + sign * field[b, rows]
        rise(b, 1).start()
        sink(b, 1).start()

    def relay(b, hop):
        rise(b, hop - 1).wait_recv()
        rise(b, hop).start()
        sink(b, hop - 1).wait_recv()
        sink(b, hop).start()

    def late_exchanges(b):
        r = b - 2
        return [
            pltpu.make_async_remote_copy(
                src_ref=source,
                dst_ref=target,
                send_sem=late_send.at[r, i],
                recv_sem=late_recv.at[r, i],
                device_id=partner,
                device_id_type=MESH,
            )
            for i, (source, target) in enumerate(
                (
                    (even.at[b, pl.ds(2, 4)], other_even.at[r]),
                    (risen.at[b], other_risen.at[r]),
                    (sunk.at[b], other_sunk.at[r]),
                )
            )
        ]

    def exchange_late(b):
        gathered(b)
        for copy in late_exchanges(b):
            copy.start()

    def all_passed_on(b):
        for hop in range(1, HOPS + 1):
            rise(b, hop).wait_send()
            sink(b, hop).wait_send()

    def combine_late(b):
        r = b - 2
        all_passed_on(b)
        for copy in late_exchanges(b):
            copy.wait()
        for i in range(4):
            even[b, i + 2] = other_even[r, i] + sign * even[b, i + 2]

        @pl.loop(0, TRAVELLING)
        def _(i):
            risen[b, i] = other_risen[r, i] + sign * risen[b, i]
            sunk[b, i] = other_sunk[r, i] + sign * sunk[b, i]

    def gathered(b):
        rise(b, HOPS).wait_recv()
        sink(b, HOPS).wait_recv()

    def terms_of(b, slab, rows):
        terms = [even[b, slab + 4, rows]]
        terms += [risen[b, START[hop] + slab + 2, rows] for hop in range(1, 4 - slab)]
        terms += [sunk[b, START[hop] + slab + 4 - hop, rows] for hop in range(1, 5 + slab)]
        return terms

    def centre_of(b):
        step = 16
        lanes = pl.ds(pl.multiple_of(b % 2 * LANES, LANES), LANES)

        @pl.loop(0, SLAB // step)
        def _(part):
            at = pl.multiple_of(part * step, step)
            for slab in NEAR:
                terms = terms_of(b, slab, pl.ds(at, step))
                for i, (which, owner) in enumerate(KEPT + SENT):
                    if which != slab:
                        continue
                    for plane in range(2):
                        base = ((row * NZ + i) * 2 + plane) * NZ
                        total = weight_ref[base] * terms[0]
                        for j in range(1, NZ):
                            total = total + weight_ref[base + j] * terms[j]
                        if owner == 0:
                            rows = pl.ds((slab + 2) * LANES + SLAB * plane + at, step)
                            spectra[b // 2, rows, lanes] = total
                        else:
                            planes[b, i - len(KEPT), pl.ds(SLAB * plane + at, step)] = total

    def send_out(b):
        for i, (slab, owner) in enumerate(SENT):
            pltpu.make_async_remote_copy(
                src_ref=planes.at[b, i],
                dst_ref=spectra.at[
                    b // 2,
                    pl.ds((slab - owner + 2) % NZ * LANES, LANES),
                    pl.ds(pl.multiple_of(b % 2 * LANES, LANES), LANES),
                ],
                send_sem=out_send.at[b],
                recv_sem=out_recv.at[b],
                device_id=peer(owner),
                device_id_type=MESH,
            ).start()

    def nth(i):
        return jnp.where(i < 5, i + 2, jnp.where(i == 5, 1, 7 * (7 - i)))

    def product(c, near):
        half = pl.ds(0 if near else WIDE // 2, WIDE // 2)
        high, low = halves(spectra[c, half, :])
        y_h[half, :] = high
        y_l[half, :] = low
        for part in range(4):
            rows = pl.ds(part * 256, 256)
            total = (
                jnp.dot(dft_h[rows, half], y_h[half, :], preferred_element_type=F32)
                + jnp.dot(dft_h[rows, half], y_l[half, :], preferred_element_type=F32)
                + jnp.dot(dft_l[rows, half], y_h[half, :], preferred_element_type=F32)
            )
            to = (c, part // 2, pl.ds(part % 2 * 256, 256))
            result[to] = total if near else result[to] + total

    def chunk(c):
        product(c, True)
        for b in (2 * c, 2 * c + 1):
            arrived(planes.at[b], out_recv.at[b])
        product(c, False)

    @pl.loop(1, NB + HOPS + 1)
    def _(i):
        for hop in range(HOPS, 1, -1):
            at = i - hop + 1

            @pl.when((at >= 0) & (at < NB))
            def _(at=at, hop=hop):
                relay(nth(at), hop)

        @pl.when((i >= RAW) & (i < NB))
        def _():
            depart(nth(i))

        pl.when(i == 2)(outermost)
        pl.when(i == 3)(build_transform)
        at = i - HOPS

        @pl.when((at >= 0) & (at < RAW))
        def _():
            exchange_late(nth(at))

        @pl.when((at >= RAW) & (at < NB))
        def _():
            b = nth(at)
            gathered(b)
            centre_of(b)
            send_out(b)

        late = i - 9

        @pl.when((late >= 0) & (late < RAW))
        def _():
            b = nth(late)
            combine_late(b)
            centre_of(b)
            send_out(b)

        @pl.when((i == 10) | (i == 12) | (i == 13))
        def _():
            chunk(jnp.where(i == 10, 2, jnp.where(i == 12, 1, 3)))

    chunk(0)

    for side in range(2):
        halo(side).wait_send()

    @pl.loop(0, NB)
    def _(b):

        @pl.when((b < 2) | (b >= 2 + RAW))
        def _():
            exchange(b).wait_send()
            all_passed_on(b)

        arrived(planes.at[b], out_send.at[b])


def write_out(result, out_hbm, sem):
    def write(c):
        return pltpu.make_async_copy(result.at[c], out_hbm.at[:, :, pl.ds(c * 256, 256)], sem.at[c])

    for c in range(4):
        write(c).start()
    for c in range(4):
        write(c).wait()


def on_device(signal, apod, coef, block_offset, fine_start):
    vmem = pl.BlockSpec(memory_space=pltpu.VMEM)
    anywhere = pl.BlockSpec(memory_space=pltpu.HBM)
    sem = pltpu.SemaphoreType.DMA
    extended = WIDE + 2 * LANES
    result = pl.pallas_call(
        kernel,
        name="f1_section",
        out_shape=jax.ShapeDtypeStruct((NB // 2, 2, ROWS, 2 * LANES), F32),
        in_specs=[anywhere] * 7,
        out_specs=vmem,
        scratch_shapes=[
            pltpu.SMEM((16 * NZ * 2 * NZ,), F32),
            pltpu.SMEM(block_offset.shape, jnp.int32),
            pltpu.VMEM((ROWS // LANES, LANES), F32),
            pltpu.VMEM((TAPS, WIDE), F32),
            pltpu.VMEM((NB, LANES), jnp.int32),
            pltpu.VMEM((ROWS, extended), F32),
            pltpu.VMEM((ROWS, extended), BF16),
            pltpu.VMEM((ROWS, extended), BF16),
            pltpu.VMEM((ROWS, LANES), F32),
            pltpu.VMEM((NB, ROWS, LANES), F32),
            pltpu.VMEM((NB, ROWS, LANES), F32),
            pltpu.VMEM((NB, NZ, SLAB, LANES), F32),
            pltpu.VMEM((NB, TRAVELLING, SLAB, LANES), F32),
            pltpu.VMEM((NB, TRAVELLING, SLAB, LANES), F32),
            pltpu.VMEM((RAW, len(NEAR), SLAB, LANES), F32),
            pltpu.VMEM((RAW, TRAVELLING, SLAB, LANES), F32),
            pltpu.VMEM((RAW, TRAVELLING, SLAB, LANES), F32),
            pltpu.VMEM((NB, len(SENT), LANES, LANES), F32),
            pltpu.VMEM((NB // 2, WIDE, 2 * LANES), F32),
            pltpu.VMEM((LANES, WIDE), F32),
            pltpu.VMEM((WIDE, WIDE), BF16),
            pltpu.VMEM((WIDE, WIDE), BF16),
            pltpu.VMEM((WIDE, 2 * LANES), BF16),
            pltpu.VMEM((WIDE, 2 * LANES), BF16),
            sem((5,)),
            sem((NB + 1,)),
            sem,
            sem((2,)),
            sem((2,)),
            sem((NB,)),
            sem((NB,)),
            sem((RAW, 3)),
            sem((RAW, 3)),
            sem((NB, HOPS)),
            sem((NB, HOPS)),
            sem((NB, HOPS)),
            sem((NB, HOPS)),
            sem((NB,)),
            sem((NB,)),
        ],
        compiler_params=pltpu.CompilerParams(
            collective_id=0, has_side_effects=True, vmem_limit_bytes=44 << 20
        ),
    )(
        *(
            pltpu.with_memory_space_constraint(value, pltpu.HBM)
            for value in (
                jnp.asarray(centre_weights()),
                block_offset,
                signal,
                jnp.asarray(transform_tables()),
                apod.reshape(ROWS // LANES, LANES),
                coef,
                fine_start.reshape(NB, LANES),
            )
        )
    )
    return pl.pallas_call(
        write_out,
        name="write_out",
        out_shape=jax.ShapeDtypeStruct((2, ROWS, WIDE), F32),
        in_specs=[vmem],
        out_specs=anywhere,
        scratch_shapes=[sem((NB // 2,))],
        compiler_params=pltpu.CompilerParams(vmem_limit_bytes=16 << 20),
    )(result)


def solution(mesh):
    placed = (P("row", "col"), P("row"), P(None, "col"), P("col"), P("col"))
    return jax.shard_map(
        on_device, mesh=mesh, in_specs=placed, out_specs=P(None, "row", "col"), check_vma=False
    )
```

```python
import functools
import math

import jax
import jax.numpy as jnp
import numpy as np
from jax import lax
from jax.experimental import pallas as pl
from jax.experimental.pallas import tpu as pltpu
from jax.sharding import PartitionSpec as P

MESH = pl.DeviceIdType.MESH
TAPS = 4
NZ = 8
NB = 8
LANES = 128
ROWS = 512
SLAB = ROWS // NZ
WIDE = NB * LANES
T1 = 8192
F32, BF16 = jnp.float32, jnp.bfloat16


def residue_of(row):
    digits = row % 2 * 8 + row // 2 % 2 * 4 + row // 4 % 2 * 2 + row // 8
    return digits


NEAR = (-2, -1, 0, 1)
HOPS = 5
RAW = 2
START = (None, 0, 5, 9, 12, 14)
TRAVELLING = 15
KEPT = tuple((slab, 0) for slab in NEAR)
SENT = ((-2, 2), (1, -2), (-2, 1), (1, -1))


def sources(slab):
    return [0] + [-hop for hop in range(1, 4 - slab)] + [hop for hop in range(1, 5 + slab)]


def centre_weights():
    table = np.zeros((16, NZ, 2, NZ))
    for row in range(16):
        x_hi, z = divmod(row, NZ)
        for i, (slab, owner) in enumerate(KEPT + SENT):
            residue = residue_of(x_hi * NZ + (z + owner) % NZ)
            for j, source in enumerate(sources(slab)):
                turn = residue * ((z + source) % NZ) % 16
                table[row, i, 0, j] = np.cos(turn * np.pi / 8)
                table[row, i, 1, j] = -np.sin(turn * np.pi / 8) if turn % 8 else 0.0
    return table.reshape(-1).astype(np.float32)


def transform_tables():
    lane = np.arange(WIDE)
    time = SLAB * (lane // LANES) + lane % SLAB
    plane = lane % LANES // SLAB
    coarse = 256 * np.arange(32)[:, None] * time
    fine = 16 * np.arange(16)[:, None] * time
    own = np.array([residue_of(row) for row in range(16)])[:, None] * time - T1 // 4 * plane
    parts = []
    for steps, size in ((coarse, 1.0), (fine, 1.0), (own, 1.0 / math.sqrt(T1))):
        angle = 2.0 * np.pi / T1 * (steps % T1)
        parts += [size * np.cos(angle), size * np.sin(angle)]
    return np.concatenate(parts).astype(np.float32)


def halves(value):
    high = value.astype(BF16)
    return high, (value - high.astype(F32)).astype(BF16)


def three_products(a_h, a_l, b_h, b_l):
    return (
        jnp.dot(a_h, b_h, preferred_element_type=F32)
        + jnp.dot(a_h, b_l, preferred_element_type=F32)
        + jnp.dot(a_l, b_h, preferred_element_type=F32)
    )


def kernel(
    weight_hbm, block_hbm, x_hbm, table_hbm, apod_hbm, coef_hbm, fine_hbm,
    result, far_h, far_l, last_h, last_l,
    weight_ref, block_ref, apod_ref, coef_ref, fine_ref, xe, xh, xl, wide_apod, field, other, even, risen, sunk,
    other_even, other_risen, other_sunk, planes, spectra, table, turned, near_h, near_l, y_h, y_l,
    small_sem, load_sem, table_sem, halo_send, halo_recv, x_send, x_recv, late_send, late_recv, up_send, up_recv, down_send, down_recv,
    out_send, out_recv,
):
    row, col = lax.axis_index("row"), lax.axis_index("col")
    x_hi, z = row // NZ, row % NZ
    cols = lax.axis_size("col")

    def peer(step):
        return (x_hi * NZ + (z + step + NZ) % NZ, col)

    partner = ((1 - x_hi) * NZ + z, col)
    up, down = (row, (col + 1) % cols), (row, (col + cols - 1) % cols)
    barrier = pltpu.get_barrier_semaphore()
    greeted = [peer(step) for step in (1, 2, -1, -2)] + [partner, up, down]
    for device in greeted:
        pl.semaphore_signal(barrier, inc=1, device_id=device, device_id_type=MESH)

    def load(t):
        return pltpu.make_async_copy(
            x_hbm.at[:, pl.ds((t - 1) * LANES, LANES)], xe.at[:, pl.ds(t * LANES, LANES)], load_sem.at[t]
        )

    small = [
        pltpu.make_async_copy(source, target, small_sem.at[i])
        for i, (source, target) in enumerate(
            (
                (apod_hbm, apod_ref),
                (coef_hbm, coef_ref),
                (fine_hbm, fine_ref),
                (block_hbm, block_ref),
                (weight_hbm, weight_ref),
            )
        )
    ]
    for t in (2, 3, 4):
        load(t).start()
    for copy in small:
        copy.start()
    for t in (5, 6, 7, 8, 1):
        load(t).start()
    tables = pltpu.make_async_copy(table_hbm, table, table_sem)
    tables.start()

    for copy in small[:4]:
        copy.wait()

    for g in range(ROWS // LANES):
        line = jnp.broadcast_to(apod_ref[g : g + 1, :], (LANES, LANES))
        wide_apod[g * LANES : (g + 1) * LANES, :] = line.T

    def split_tile(t):
        at = pl.ds(t * LANES, LANES)
        high, low = halves(xe[:, at] * wide_apod[...])
        xh[:, at] = high
        xl[:, at] = low

    def stencil_block(b):
        at, window = pl.ds(b * LANES, LANES), pl.ds(b * LANES, 3 * LANES)
        shape = (3 * LANES, LANES)
        lane = lax.broadcasted_iota(jnp.int32, (1, LANES), 1)
        first = lane + LANES + fine_ref[b : b + 1, :]
        for part in range(4):
            inside = lane // 32 == part
            first = first + jnp.where(inside, block_ref[4 * b + part], 0)
        tap = lax.broadcasted_iota(jnp.int32, shape, 0) - first
        band = jnp.zeros(shape, F32)
        for q in range(TAPS):
            band = jnp.where(tap == q, coef_ref[q : q + 1, at], band)
        band_h, band_l = halves(band)
        xw = xh[:, window]
        field[b] = three_products(xw, xl[:, window], band_h, band_l)

    def exchange(b):
        return pltpu.make_async_remote_copy(
            src_ref=field.at[b],
            dst_ref=other.at[b],
            send_sem=x_send.at[b],
            recv_sem=x_recv.at[b],
            device_id=partner,
            device_id_type=MESH,
        )

    def rise(b, hop):
        if hop == 1:
            source = even.at[b, pl.ds(3, 5)]
        else:
            source = risen.at[b, pl.ds(START[hop - 1] + 1, 6 - hop)]
        return pltpu.make_async_remote_copy(
            src_ref=source,
            dst_ref=risen.at[b, pl.ds(START[hop], 6 - hop)],
            send_sem=up_send.at[b, hop - 1],
            recv_sem=up_recv.at[b, hop - 1],
            device_id=peer(1),
            device_id_type=MESH,
        )

    def sink(b, hop):
        if hop == 1:
            source = even.at[b, pl.ds(0, 5)]
        else:
            source = sunk.at[b, pl.ds(START[hop - 1], 6 - hop)]
        return pltpu.make_async_remote_copy(
            src_ref=source,
            dst_ref=sunk.at[b, pl.ds(START[hop], 6 - hop)],
            send_sem=down_send.at[b, hop - 1],
            recv_sem=down_recv.at[b, hop - 1],
            device_id=peer(-1),
            device_id_type=MESH,
        )

    def depart_raw(b):
        for i in range(NZ):
            rows = pl.ds(pl.multiple_of((z + i + 4) % NZ * SLAB, SLAB), SLAB)
            even[b, i] = field[b, rows]
        rise(b, 1).start()
        sink(b, 1).start()

    def halo(side):
        return pltpu.make_async_remote_copy(
            src_ref=x_hbm.at[:, pl.ds((WIDE - LANES) * (1 - side), LANES)],
            dst_ref=xe.at[:, pl.ds((LANES + WIDE) * side, LANES)],
            send_sem=halo_send.at[side],
            recv_sem=halo_recv.at[side],
            device_id=(up, down)[side],
            device_id_type=MESH,
        )

    for t in (2, 3):
        load(t).wait()
        split_tile(t)
    for b in range(2, 7):
        load(b + 2).wait()
        split_tile(b + 2)
        stencil_block(b)
        if b == 2:
            pl.semaphore_wait(barrier, len(greeted))
        if b < 2 + RAW:
            depart_raw(b)
        else:
            exchange(b).start()
        if b == 3:
            for side in range(2):
                halo(side).start()
    load(1).wait()
    split_tile(1)
    stencil_block(1)
    exchange(1).start()

    small[4].wait()

    def outermost():
        for side in range(2):
            halo(side).wait_recv()

        @pl.when(col == 0)
        def _():
            xe[:, :LANES] = jnp.zeros((ROWS, LANES), F32)

        @pl.when(col == cols - 1)
        def _():
            xe[:, LANES + WIDE :] = jnp.zeros((ROWS, LANES), F32)

        split_tile(NB + 1)
        stencil_block(7)
        exchange(7).start()
        split_tile(0)
        stencil_block(0)
        exchange(0).start()

    def build_transform():
        tables.wait()
        own_c, own_s = table[pl.ds(96 + row, 1), :], table[pl.ds(112 + row, 1), :]
        p = table[64:80, :] * own_c - table[80:96, :] * own_s
        q = table[80:96, :] * own_c + table[64:80, :] * own_s
        table[64:80, :] = p
        table[80:96, :] = q

        for j in range(NZ):
            lanes = pl.ds(pl.multiple_of((z + j - 2 + NZ) % NZ * LANES, LANES), LANES)
            turned[:, j * LANES : (j + 1) * LANES] = table[:96, lanes]

        @pl.loop(0, 32)
        def _(k):
            c, s = turned[pl.ds(k, 1), :], turned[pl.ds(32 + k, 1), :]
            p, q = turned[64:80, :], turned[80:96, :]
            top = halves(c * p - s * q)
            low = halves(-(s * p + c * q))
            for first, (high, rest) in ((0, top), (ROWS, low)):
                rows = pl.ds(pl.multiple_of(first + k * 16, 16), 16)
                near_h[rows, :], far_h[rows, :] = high[:, : WIDE // 2], high[:, WIDE // 2 :]
                near_l[rows, :], far_l[rows, :] = rest[:, : WIDE // 2], rest[:, WIDE // 2 :]

    def arrived(ref, sem):
        pltpu.make_async_copy(ref, ref, sem).wait()

    sign = (1 - 2 * x_hi).astype(F32)

    def depart(b):
        exchange(b).wait_recv()
        for i in range(NZ):
            rows = pl.ds(pl.multiple_of((z + i + 4) % NZ * SLAB, SLAB), SLAB)
            even[b, i] = other[b, rows] + sign * field[b, rows]
        rise(b, 1).start()
        sink(b, 1).start()

    def relay(b, hop):
        rise(b, hop - 1).wait_recv()
        rise(b, hop).start()
        sink(b, hop - 1).wait_recv()
        sink(b, hop).start()

    def late_exchanges(b):
        r = b - 2
        return [
            pltpu.make_async_remote_copy(
                src_ref=source,
                dst_ref=target,
                send_sem=late_send.at[r, i],
                recv_sem=late_recv.at[r, i],
                device_id=partner,
                device_id_type=MESH,
            )
            for i, (source, target) in enumerate(
                (
                    (even.at[b, pl.ds(2, 4)], other_even.at[r]),
                    (risen.at[b], other_risen.at[r]),
                    (sunk.at[b], other_sunk.at[r]),
                )
            )
        ]

    def exchange_late(b):
        gathered(b)
        for copy in late_exchanges(b):
            copy.start()

    def all_passed_on(b):
        for hop in range(1, HOPS + 1):
            rise(b, hop).wait_send()
            sink(b, hop).wait_send()

    def combine_late(b):
        r = b - 2
        all_passed_on(b)
        for copy in late_exchanges(b):
            copy.wait()
        for i in range(4):
            even[b, i + 2] = other_even[r, i] + sign * even[b, i + 2]

        @pl.loop(0, TRAVELLING)
        def _(i):
            risen[b, i] = other_risen[r, i] + sign * risen[b, i]
            sunk[b, i] = other_sunk[r, i] + sign * sunk[b, i]

    def gathered(b):
        rise(b, HOPS).wait_recv()
        sink(b, HOPS).wait_recv()

    def terms_of(b, slab, rows):
        terms = [even[b, slab + 4, rows]]
        terms += [risen[b, START[hop] + slab + 2, rows] for hop in range(1, 4 - slab)]
        terms += [sunk[b, START[hop] + slab + 4 - hop, rows] for hop in range(1, 5 + slab)]
        return terms

    def centre_of(b):
        step = 16
        lanes = pl.ds(pl.multiple_of(b % 2 * LANES, LANES), LANES)

        @pl.loop(0, SLAB // step)
        def _(part):
            at = pl.multiple_of(part * step, step)
            for slab in NEAR:
                terms = terms_of(b, slab, pl.ds(at, step))
                for i, (which, owner) in enumerate(KEPT + SENT):
                    if which != slab:
                        continue
                    for plane in range(2):
                        base = ((row * NZ + i) * 2 + plane) * NZ
                        total = weight_ref[base] * terms[0]
                        for j in range(1, NZ):
                            total = total + weight_ref[base + j] * terms[j]
                        if owner == 0:
                            rows = pl.ds((slab + 2) * LANES + SLAB * plane + at, step)
                            spectra[b // 2, rows, lanes] = total
                        else:
                            planes[b, i - len(KEPT), pl.ds(SLAB * plane + at, step)] = total

    def send_out(b):
        for i, (slab, owner) in enumerate(SENT):
            pltpu.make_async_remote_copy(
                src_ref=planes.at[b, i],
                dst_ref=spectra.at[
                    b // 2,
                    pl.ds((slab - owner + 2) % NZ * LANES, LANES),
                    pl.ds(pl.multiple_of(b % 2 * LANES, LANES), LANES),
                ],
                send_sem=out_send.at[b],
                recv_sem=out_recv.at[b],
                device_id=peer(owner),
                device_id_type=MESH,
            ).start()

    def nth(i):
        return jnp.where(i < 5, i + 2, jnp.where(i == 5, 1, 7 * (7 - i)))

    def product(c, near):
        half = pl.ds(0 if near else WIDE // 2, WIDE // 2)
        y_h[...], y_l[...] = halves(spectra[c, half, :])
        for part in range(4):
            rows = pl.ds(part * 256, 256)
            at_h, at_l = (near_h[rows, :], near_l[rows, :]) if near else (far_h[rows, :], far_l[rows, :])
            total = three_products(at_h, at_l, y_h[...], y_l[...])
            to = (c, part // 2, pl.ds(part % 2 * 256, 256))
            result[to] = total if near else result[to] + total

    def owned(c):
        for b in (2 * c, 2 * c + 1):
            arrived(planes.at[b], out_recv.at[b])

    def chunk(c):
        product(c, True)
        owned(c)
        product(c, False)

    @pl.loop(1, NB + HOPS + 1)
    def _(i):
        for hop in range(HOPS, 1, -1):
            at = i - hop + 1

            @pl.when((at >= 0) & (at < NB))
            def _(at=at, hop=hop):
                relay(nth(at), hop)

        @pl.when((i >= RAW) & (i < NB))
        def _():
            depart(nth(i))

        pl.when(i == 2)(outermost)
        pl.when(i == 3)(build_transform)
        at = i - HOPS

        @pl.when((at >= 0) & (at < RAW))
        def _():
            exchange_late(nth(at))

        @pl.when((at >= RAW) & (at < NB))
        def _():
            b = nth(at)
            gathered(b)
            centre_of(b)
            send_out(b)

        late = i - 8

        @pl.when((late >= 0) & (late < RAW))
        def _():
            b = nth(late)
            combine_late(b)
            centre_of(b)
            send_out(b)

        @pl.when((i == 10) | (i == 12) | (i == 13))
        def _():
            chunk(jnp.where(i == 10, 2, jnp.where(i == 12, 1, 3)))

    product(0, True)
    owned(0)
    last_h[...], last_l[...] = halves(spectra[0, pl.ds(WIDE // 2, WIDE // 2), :])

    for side in range(2):
        halo(side).wait_send()

    @pl.loop(0, NB)
    def _(b):

        @pl.when((b < 2) | (b >= 2 + RAW))
        def _():
            exchange(b).wait_send()
            all_passed_on(b)

        arrived(planes.at[b], out_send.at[b])


def write_out(result, far_h, far_l, last_h, last_l, out_hbm, last, sem):
    def write(c):
        return pltpu.make_async_copy(result.at[c], out_hbm.at[:, :, pl.ds(c * 256, 256)], sem.at[c])

    def write_part(part):
        at = (part // 2, pl.ds(part % 2 * 256, 256))
        return pltpu.make_async_copy(last.at[at], out_hbm.at[*at, pl.ds(0, 256)], sem.at[4 + part])

    for c in range(1, 4):
        write(c).start()
    for part in range(4):
        at, rows = (part // 2, pl.ds(part % 2 * 256, 256)), pl.ds(part * 256, 256)
        total = three_products(far_h[rows, :], far_l[rows, :], last_h[...], last_l[...])
        last[at] = result[0, *at] + total
        write_part(part).start()
    for c in range(1, 4):
        write(c).wait()
    for part in range(4):
        write_part(part).wait()


def on_device(signal, apod, coef, block_offset, fine_start):
    vmem = pl.BlockSpec(memory_space=pltpu.VMEM)
    anywhere = pl.BlockSpec(memory_space=pltpu.HBM)
    sem = pltpu.SemaphoreType.DMA
    extended = WIDE + 2 * LANES
    done = pl.pallas_call(
        kernel,
        name="f1_section",
        out_shape=[
            jax.ShapeDtypeStruct((NB // 2, 2, ROWS, 2 * LANES), F32),
            jax.ShapeDtypeStruct((WIDE, WIDE // 2), BF16),
            jax.ShapeDtypeStruct((WIDE, WIDE // 2), BF16),
            jax.ShapeDtypeStruct((WIDE // 2, 2 * LANES), BF16),
            jax.ShapeDtypeStruct((WIDE // 2, 2 * LANES), BF16),
        ],
        in_specs=[anywhere] * 7,
        out_specs=[vmem] * 5,
        scratch_shapes=[
            pltpu.SMEM((16 * NZ * 2 * NZ,), F32),
            pltpu.SMEM(block_offset.shape, jnp.int32),
            pltpu.VMEM((ROWS // LANES, LANES), F32),
            pltpu.VMEM((TAPS, WIDE), F32),
            pltpu.VMEM((NB, LANES), jnp.int32),
            pltpu.VMEM((ROWS, extended), F32),
            pltpu.VMEM((ROWS, extended), BF16),
            pltpu.VMEM((ROWS, extended), BF16),
            pltpu.VMEM((ROWS, LANES), F32),
            pltpu.VMEM((NB, ROWS, LANES), F32),
            pltpu.VMEM((NB, ROWS, LANES), F32),
            pltpu.VMEM((NB, NZ, SLAB, LANES), F32),
            pltpu.VMEM((NB, TRAVELLING, SLAB, LANES), F32),
            pltpu.VMEM((NB, TRAVELLING, SLAB, LANES), F32),
            pltpu.VMEM((RAW, len(NEAR), SLAB, LANES), F32),
            pltpu.VMEM((RAW, TRAVELLING, SLAB, LANES), F32),
            pltpu.VMEM((RAW, TRAVELLING, SLAB, LANES), F32),
            pltpu.VMEM((NB, len(SENT), LANES, LANES), F32),
            pltpu.VMEM((NB // 2, WIDE, 2 * LANES), F32),
            pltpu.VMEM((LANES, WIDE), F32),
            pltpu.VMEM((96, WIDE), F32),
            pltpu.VMEM((WIDE, WIDE // 2), BF16),
            pltpu.VMEM((WIDE, WIDE // 2), BF16),
            pltpu.VMEM((WIDE // 2, 2 * LANES), BF16),
            pltpu.VMEM((WIDE // 2, 2 * LANES), BF16),
            sem((5,)),
            sem((NB + 1,)),
            sem,
            sem((2,)),
            sem((2,)),
            sem((NB,)),
            sem((NB,)),
            sem((RAW, 3)),
            sem((RAW, 3)),
            sem((NB, HOPS)),
            sem((NB, HOPS)),
            sem((NB, HOPS)),
            sem((NB, HOPS)),
            sem((NB,)),
            sem((NB,)),
        ],
        compiler_params=pltpu.CompilerParams(
            collective_id=0, has_side_effects=True, vmem_limit_bytes=44 << 20
        ),
    )(
        *(
            pltpu.with_memory_space_constraint(value, pltpu.HBM)
            for value in (
                jnp.asarray(centre_weights()),
                block_offset,
                signal,
                jnp.asarray(transform_tables()),
                apod.reshape(ROWS // LANES, LANES),
                coef,
                fine_start.reshape(NB, LANES),
            )
        )
    )
    return pl.pallas_call(
        write_out,
        name="write_out",
        out_shape=jax.ShapeDtypeStruct((2, ROWS, WIDE), F32),
        in_specs=[vmem] * 5,
        out_specs=anywhere,
        scratch_shapes=[pltpu.VMEM((2, ROWS, 2 * LANES), F32), sem((8,))],
        compiler_params=pltpu.CompilerParams(vmem_limit_bytes=16 << 20),
    )(*done)


def solution(mesh):
    placed = (P("row", "col"), P("row"), P(None, "col"), P("col"), P("col"))
    return jax.shard_map(
        on_device, mesh=mesh, in_specs=placed, out_specs=P(None, "row", "col"), check_vma=False
    )
```

```python
import functools
import math

import jax
import jax.numpy as jnp
import numpy as np
from jax import lax
from jax.experimental import pallas as pl
from jax.experimental.pallas import tpu as pltpu
from jax.sharding import PartitionSpec as P

MESH = pl.DeviceIdType.MESH
TAPS = 4
NZ = 8
NB = 8
LANES = 128
ROWS = 512
SLAB = ROWS // NZ
WIDE = NB * LANES
T1 = 8192
F32, BF16 = jnp.float32, jnp.bfloat16


def residue_of(row):
    digits = row % 2 * 8 + row // 2 % 2 * 4 + row // 4 % 2 * 2 + row // 8
    return digits


NEAR = (-2, -1, 0, 1)
HOPS = 5
RAW = 2
START = (None, 0, 5, 9, 12, 14)
TRAVELLING = 15
KEPT = tuple((slab, 0) for slab in NEAR)
SENT = ((-2, 2), (1, -2), (-2, 1), (1, -1))


def sources(slab):
    return [0] + [-hop for hop in range(1, 4 - slab)] + [hop for hop in range(1, 5 + slab)]


def centre_weights():
    table = np.zeros((16, NZ, 2, NZ))
    for row in range(16):
        x_hi, z = divmod(row, NZ)
        for i, (slab, owner) in enumerate(KEPT + SENT):
            residue = residue_of(x_hi * NZ + (z + owner) % NZ)
            for j, source in enumerate(sources(slab)):
                turn = residue * ((z + source) % NZ) % 16
                table[row, i, 0, j] = np.cos(turn * np.pi / 8)
                table[row, i, 1, j] = -np.sin(turn * np.pi / 8) if turn % 8 else 0.0
    return table.reshape(-1).astype(np.float32)


def transform_tables():
    lane = np.arange(WIDE)
    time = SLAB * (lane // LANES) + lane % SLAB
    plane = lane % LANES // SLAB
    coarse = 256 * np.arange(32)[:, None] * time
    fine = 16 * np.arange(16)[:, None] * time
    own = np.array([residue_of(row) for row in range(16)])[:, None] * time - T1 // 4 * plane
    parts = []
    for steps, size in ((coarse, 1.0), (fine, 1.0), (own, 1.0 / math.sqrt(T1))):
        angle = 2.0 * np.pi / T1 * (steps % T1)
        parts += [size * np.cos(angle), size * np.sin(angle)]
    return np.concatenate(parts).astype(np.float32)


def halves(value):
    high = value.astype(BF16)
    return high, (value - high.astype(F32)).astype(BF16)


def three_products(a_h, a_l, b_h, b_l):
    return (
        jnp.dot(a_h, b_h, preferred_element_type=F32)
        + jnp.dot(a_h, b_l, preferred_element_type=F32)
        + jnp.dot(a_l, b_h, preferred_element_type=F32)
    )


def kernel(
    weight_hbm, block_hbm, x_hbm, table_hbm, apod_hbm, coef_hbm, fine_hbm,
    result, far_h, far_l, last_h, last_l,
    weight_ref, block_ref, apod_ref, coef_ref, fine_ref, xe, xh, xl, wide_apod, field, other, even, risen, sunk,
    other_even, other_risen, other_sunk, planes, spectra, table, turned, near_h, near_l, y_h, y_l,
    small_sem, load_sem, table_sem, halo_send, halo_recv, x_send, x_recv, late_send, late_recv, up_send, up_recv, down_send, down_recv,
    out_send, out_recv,
):
    row, col = lax.axis_index("row"), lax.axis_index("col")
    x_hi, z = row // NZ, row % NZ
    cols = lax.axis_size("col")

    def peer(step):
        return (x_hi * NZ + (z + step + NZ) % NZ, col)

    partner = ((1 - x_hi) * NZ + z, col)
    up, down = (row, (col + 1) % cols), (row, (col + cols - 1) % cols)
    barrier = pltpu.get_barrier_semaphore()
    greeted = [peer(step) for step in (1, 2, -1, -2)] + [partner, up, down]
    for device in greeted:
        pl.semaphore_signal(barrier, inc=1, device_id=device, device_id_type=MESH)

    def load(t):
        return pltpu.make_async_copy(
            x_hbm.at[:, pl.ds((t - 1) * LANES, LANES)], xe.at[:, pl.ds(t * LANES, LANES)], load_sem.at[t]
        )

    small = [
        pltpu.make_async_copy(source, target, small_sem.at[i])
        for i, (source, target) in enumerate(
            (
                (apod_hbm, apod_ref),
                (coef_hbm, coef_ref),
                (fine_hbm, fine_ref),
                (block_hbm, block_ref),
                (weight_hbm, weight_ref),
            )
        )
    ]
    for t in (2, 3, 4):
        load(t).start()
    for copy in small:
        copy.start()
    for t in (5, 6, 7, 8, 1):
        load(t).start()
    tables = pltpu.make_async_copy(table_hbm, table, table_sem)
    tables.start()

    for copy in small[:4]:
        copy.wait()

    for g in range(ROWS // LANES):
        line = jnp.broadcast_to(apod_ref[g : g + 1, :], (LANES, LANES))
        wide_apod[g * LANES : (g + 1) * LANES, :] = line.T

    def split_tile(t):
        at = pl.ds(t * LANES, LANES)
        high, low = halves(xe[:, at] * wide_apod[...])
        xh[:, at] = high
        xl[:, at] = low

    def stencil_block(b):
        at, window = pl.ds(b * LANES, LANES), pl.ds(b * LANES, 3 * LANES)
        shape = (3 * LANES, LANES)
        lane = lax.broadcasted_iota(jnp.int32, (1, LANES), 1)
        first = lane + LANES + fine_ref[b : b + 1, :]
        for part in range(4):
            inside = lane // 32 == part
            first = first + jnp.where(inside, block_ref[4 * b + part], 0)
        tap = lax.broadcasted_iota(jnp.int32, shape, 0) - first
        band = jnp.zeros(shape, F32)
        for q in range(TAPS):
            band = jnp.where(tap == q, coef_ref[q : q + 1, at], band)
        band_h, band_l = halves(band)
        xw = xh[:, window]
        field[b] = three_products(xw, xl[:, window], band_h, band_l)

    def exchange(b):
        return pltpu.make_async_remote_copy(
            src_ref=field.at[b],
            dst_ref=other.at[b],
            send_sem=x_send.at[b],
            recv_sem=x_recv.at[b],
            device_id=partner,
            device_id_type=MESH,
        )

    def rise(b, hop):
        if hop == 1:
            source = even.at[b, pl.ds(3, 5)]
        else:
            source = risen.at[b, pl.ds(START[hop - 1] + 1, 6 - hop)]
        return pltpu.make_async_remote_copy(
            src_ref=source,
            dst_ref=risen.at[b, pl.ds(START[hop], 6 - hop)],
            send_sem=up_send.at[b, hop - 1],
            recv_sem=up_recv.at[b, hop - 1],
            device_id=peer(1),
            device_id_type=MESH,
        )

    def sink(b, hop):
        if hop == 1:
            source = even.at[b, pl.ds(0, 5)]
        else:
            source = sunk.at[b, pl.ds(START[hop - 1], 6 - hop)]
        return pltpu.make_async_remote_copy(
            src_ref=source,
            dst_ref=sunk.at[b, pl.ds(START[hop], 6 - hop)],
            send_sem=down_send.at[b, hop - 1],
            recv_sem=down_recv.at[b, hop - 1],
            device_id=peer(-1),
            device_id_type=MESH,
        )

    def depart_raw(b):
        for i in range(NZ):
            rows = pl.ds(pl.multiple_of((z + i + 4) % NZ * SLAB, SLAB), SLAB)
            even[b, i] = field[b, rows]
        rise(b, 1).start()
        sink(b, 1).start()

    def halo(side):
        return pltpu.make_async_remote_copy(
            src_ref=x_hbm.at[:, pl.ds((WIDE - LANES) * (1 - side), LANES)],
            dst_ref=xe.at[:, pl.ds((LANES + WIDE) * side, LANES)],
            send_sem=halo_send.at[side],
            recv_sem=halo_recv.at[side],
            device_id=(up, down)[side],
            device_id_type=MESH,
        )

    ready = []
    for b in (2, 4, 3, 5, 6):
        for t in range(b, b + 3):
            if t not in ready:
                load(t).wait()
                split_tile(t)
                ready.append(t)
        stencil_block(b)
        if b == 2:
            pl.semaphore_wait(barrier, len(greeted))
        if b < 2 + RAW:
            depart_raw(b)
        else:
            exchange(b).start()
    for side in range(2):
        halo(side).start()
    load(1).wait()
    split_tile(1)
    stencil_block(1)
    exchange(1).start()

    small[4].wait()

    def outermost():
        for side in range(2):
            halo(side).wait_recv()

        @pl.when(col == 0)
        def _():
            xe[:, :LANES] = jnp.zeros((ROWS, LANES), F32)

        @pl.when(col == cols - 1)
        def _():
            xe[:, LANES + WIDE :] = jnp.zeros((ROWS, LANES), F32)

        split_tile(NB + 1)
        stencil_block(7)
        exchange(7).start()
        split_tile(0)
        stencil_block(0)
        exchange(0).start()

    def build_transform():
        tables.wait()
        own_c, own_s = table[pl.ds(96 + row, 1), :], table[pl.ds(112 + row, 1), :]
        p = table[64:80, :] * own_c - table[80:96, :] * own_s
        q = table[80:96, :] * own_c + table[64:80, :] * own_s
        table[64:80, :] = p
        table[80:96, :] = q

        for j in range(NZ):
            lanes = pl.ds(pl.multiple_of((z + j - 2 + NZ) % NZ * LANES, LANES), LANES)
            turned[:, j * LANES : (j + 1) * LANES] = table[:96, lanes]

        @pl.loop(0, 32)
        def _(k):
            c, s = turned[pl.ds(k, 1), :], turned[pl.ds(32 + k, 1), :]
            p, q = turned[64:80, :], turned[80:96, :]
            top = halves(c * p - s * q)
            low = halves(-(s * p + c * q))
            for first, (high, rest) in ((0, top), (ROWS, low)):
                rows = pl.ds(pl.multiple_of(first + k * 16, 16), 16)
                near_h[rows, :], far_h[rows, :] = high[:, : WIDE // 2], high[:, WIDE // 2 :]
                near_l[rows, :], far_l[rows, :] = rest[:, : WIDE // 2], rest[:, WIDE // 2 :]

    def arrived(ref, sem):
        pltpu.make_async_copy(ref, ref, sem).wait()

    sign = (1 - 2 * x_hi).astype(F32)

    def depart(b):
        exchange(b).wait_recv()
        for i in range(NZ):
            rows = pl.ds(pl.multiple_of((z + i + 4) % NZ * SLAB, SLAB), SLAB)
            even[b, i] = other[b, rows] + sign * field[b, rows]
        rise(b, 1).start()
        sink(b, 1).start()

    def relay(b, hop):
        rise(b, hop - 1).wait_recv()
        rise(b, hop).start()
        sink(b, hop - 1).wait_recv()
        sink(b, hop).start()

    def late_exchanges(b):
        r = b - 2
        return [
            pltpu.make_async_remote_copy(
                src_ref=source,
                dst_ref=target,
                send_sem=late_send.at[r, i],
                recv_sem=late_recv.at[r, i],
                device_id=partner,
                device_id_type=MESH,
            )
            for i, (source, target) in enumerate(
                (
                    (even.at[b, pl.ds(2, 4)], other_even.at[r]),
                    (risen.at[b, pl.ds(0, 4)], other_risen.at[r, pl.ds(0, 4)]),
                    (risen.at[b, pl.ds(5, 10)], other_risen.at[r, pl.ds(5, 10)]),
                    (sunk.at[b, pl.ds(1, 14)], other_sunk.at[r, pl.ds(1, 14)]),
                )
            )
        ]

    def exchange_late(b):
        gathered(b)
        for copy in late_exchanges(b):
            copy.start()

    def all_passed_on(b):
        for hop in range(1, HOPS + 1):
            rise(b, hop).wait_send()
            sink(b, hop).wait_send()

    def combine_late(b):
        r = b - 2
        all_passed_on(b)
        for copy in late_exchanges(b):
            copy.wait()
        for i in range(4):
            even[b, i + 2] = other_even[r, i] + sign * even[b, i + 2]

        @pl.loop(0, TRAVELLING - 1)
        def _(i):
            up, down = jnp.where(i < 4, i, i + 1), i + 1
            risen[b, up] = other_risen[r, up] + sign * risen[b, up]
            sunk[b, down] = other_sunk[r, down] + sign * sunk[b, down]

    def gathered(b):
        rise(b, HOPS).wait_recv()
        sink(b, HOPS).wait_recv()

    def terms_of(b, slab, rows):
        terms = [even[b, slab + 4, rows]]
        terms += [risen[b, START[hop] + slab + 2, rows] for hop in range(1, 4 - slab)]
        terms += [sunk[b, START[hop] + slab + 4 - hop, rows] for hop in range(1, 5 + slab)]
        return terms

    def centre_of(b):
        step = 16
        lanes = pl.ds(pl.multiple_of(b % 2 * LANES, LANES), LANES)

        @pl.loop(0, SLAB // step)
        def _(part):
            at = pl.multiple_of(part * step, step)
            for slab in NEAR:
                terms = terms_of(b, slab, pl.ds(at, step))
                for i, (which, owner) in enumerate(KEPT + SENT):
                    if which != slab:
                        continue
                    for plane in range(2):
                        base = ((row * NZ + i) * 2 + plane) * NZ
                        total = weight_ref[base] * terms[0]
                        for j in range(1, NZ):
                            total = total + weight_ref[base + j] * terms[j]
                        if owner == 0:
                            rows = pl.ds((slab + 2) * LANES + SLAB * plane + at, step)
                            spectra[b // 2, rows, lanes] = total
                        else:
                            planes[b, i - len(KEPT), pl.ds(SLAB * plane + at, step)] = total

    def send_out(b):
        for i, (slab, owner) in enumerate(SENT):
            pltpu.make_async_remote_copy(
                src_ref=planes.at[b, i],
                dst_ref=spectra.at[
                    b // 2,
                    pl.ds((slab - owner + 2) % NZ * LANES, LANES),
                    pl.ds(pl.multiple_of(b % 2 * LANES, LANES), LANES),
                ],
                send_sem=out_send.at[b],
                recv_sem=out_recv.at[b],
                device_id=peer(owner),
                device_id_type=MESH,
            ).start()

    def nth(i):
        return jnp.where(i < 5, i + 2, jnp.where(i == 5, 1, 7 * (7 - i)))

    def product(c, near):
        half = pl.ds(0 if near else WIDE // 2, WIDE // 2)
        y_h[...], y_l[...] = halves(spectra[c, half, :])
        for part in range(4):
            rows = pl.ds(part * 256, 256)
            at_h, at_l = (near_h[rows, :], near_l[rows, :]) if near else (far_h[rows, :], far_l[rows, :])
            total = three_products(at_h, at_l, y_h[...], y_l[...])
            to = (c, part // 2, pl.ds(part % 2 * 256, 256))
            result[to] = total if near else result[to] + total

    def owned(c):
        for b in (2 * c, 2 * c + 1):
            arrived(planes.at[b], out_recv.at[b])

    def chunk(c):
        product(c, True)
        owned(c)
        product(c, False)

    @pl.loop(1, NB + HOPS + 1)
    def _(i):
        for hop in range(HOPS, 1, -1):
            at = i - hop + 1

            @pl.when((at >= 0) & (at < NB))
            def _(at=at, hop=hop):
                relay(nth(at), hop)

        @pl.when((i >= RAW) & (i < NB))
        def _():
            depart(nth(i))

        pl.when(i == 4)(outermost)
        pl.when(i == 3)(build_transform)
        at = i - HOPS

        @pl.when((at >= 0) & (at < RAW))
        def _():
            exchange_late(nth(at))

        @pl.when((at >= RAW) & (at < NB))
        def _():
            b = nth(at)
            gathered(b)
            centre_of(b)
            send_out(b)

        late = i - 8

        @pl.when((late >= 0) & (late < RAW))
        def _():
            b = nth(late)
            combine_late(b)
            centre_of(b)
            send_out(b)

        @pl.when((i == 10) | (i == 11) | (i == 13))
        def _():
            chunk(jnp.where(i == 10, 2, jnp.where(i == 11, 1, 3)))

    product(0, True)
    owned(0)
    last_h[...], last_l[...] = halves(spectra[0, pl.ds(WIDE // 2, WIDE // 2), :])

    for side in range(2):
        halo(side).wait_send()

    @pl.loop(0, NB)
    def _(b):

        @pl.when((b < 2) | (b >= 2 + RAW))
        def _():
            exchange(b).wait_send()
            all_passed_on(b)

        arrived(planes.at[b], out_send.at[b])


def write_out(result, far_h, far_l, last_h, last_l, out_hbm, last, sem):
    def write(c):
        return pltpu.make_async_copy(result.at[c], out_hbm.at[:, :, pl.ds(c * 256, 256)], sem.at[c])

    def write_part(part):
        at = (part // 2, pl.ds(part % 2 * 256, 256))
        return pltpu.make_async_copy(last.at[at], out_hbm.at[*at, pl.ds(0, 256)], sem.at[4 + part])

    for c in range(1, 4):
        write(c).start()
    for part in range(4):
        at, rows = (part // 2, pl.ds(part % 2 * 256, 256)), pl.ds(part * 256, 256)
        total = three_products(far_h[rows, :], far_l[rows, :], last_h[...], last_l[...])
        last[at] = result[0, *at] + total
        write_part(part).start()
    for c in range(1, 4):
        write(c).wait()
    for part in range(4):
        write_part(part).wait()


def on_device(signal, apod, coef, block_offset, fine_start):
    vmem = pl.BlockSpec(memory_space=pltpu.VMEM)
    anywhere = pl.BlockSpec(memory_space=pltpu.HBM)
    sem = pltpu.SemaphoreType.DMA
    extended = WIDE + 2 * LANES
    done = pl.pallas_call(
        kernel,
        name="f1_section",
        out_shape=[
            jax.ShapeDtypeStruct((NB // 2, 2, ROWS, 2 * LANES), F32),
            jax.ShapeDtypeStruct((WIDE, WIDE // 2), BF16),
            jax.ShapeDtypeStruct((WIDE, WIDE // 2), BF16),
            jax.ShapeDtypeStruct((WIDE // 2, 2 * LANES), BF16),
            jax.ShapeDtypeStruct((WIDE // 2, 2 * LANES), BF16),
        ],
        in_specs=[anywhere] * 7,
        out_specs=[vmem] * 5,
        scratch_shapes=[
            pltpu.SMEM((16 * NZ * 2 * NZ,), F32),
            pltpu.SMEM(block_offset.shape, jnp.int32),
            pltpu.VMEM((ROWS // LANES, LANES), F32),
            pltpu.VMEM((TAPS, WIDE), F32),
            pltpu.VMEM((NB, LANES), jnp.int32),
            pltpu.VMEM((ROWS, extended), F32),
            pltpu.VMEM((ROWS, extended), BF16),
            pltpu.VMEM((ROWS, extended), BF16),
            pltpu.VMEM((ROWS, LANES), F32),
            pltpu.VMEM((NB, ROWS, LANES), F32),
            pltpu.VMEM((NB, ROWS, LANES), F32),
            pltpu.VMEM((NB, NZ, SLAB, LANES), F32),
            pltpu.VMEM((NB, TRAVELLING, SLAB, LANES), F32),
            pltpu.VMEM((NB, TRAVELLING, SLAB, LANES), F32),
            pltpu.VMEM((RAW, len(NEAR), SLAB, LANES), F32),
            pltpu.VMEM((RAW, TRAVELLING, SLAB, LANES), F32),
            pltpu.VMEM((RAW, TRAVELLING, SLAB, LANES), F32),
            pltpu.VMEM((NB, len(SENT), LANES, LANES), F32),
            pltpu.VMEM((NB // 2, WIDE, 2 * LANES), F32),
            pltpu.VMEM((LANES, WIDE), F32),
            pltpu.VMEM((96, WIDE), F32),
            pltpu.VMEM((WIDE, WIDE // 2), BF16),
            pltpu.VMEM((WIDE, WIDE // 2), BF16),
            pltpu.VMEM((WIDE // 2, 2 * LANES), BF16),
            pltpu.VMEM((WIDE // 2, 2 * LANES), BF16),
            sem((5,)),
            sem((NB + 1,)),
            sem,
            sem((2,)),
            sem((2,)),
            sem((NB,)),
            sem((NB,)),
            sem((RAW, 4)),
            sem((RAW, 4)),
            sem((NB, HOPS)),
            sem((NB, HOPS)),
            sem((NB, HOPS)),
            sem((NB, HOPS)),
            sem((NB,)),
            sem((NB,)),
        ],
        compiler_params=pltpu.CompilerParams(
            collective_id=0, has_side_effects=True, vmem_limit_bytes=44 << 20
        ),
    )(
        *(
            pltpu.with_memory_space_constraint(value, pltpu.HBM)
            for value in (
                jnp.asarray(centre_weights()),
                block_offset,
                signal,
                jnp.asarray(transform_tables()),
                apod.reshape(ROWS // LANES, LANES),
                coef,
                fine_start.reshape(NB, LANES),
            )
        )
    )
    return pl.pallas_call(
        write_out,
        name="write_out",
        out_shape=jax.ShapeDtypeStruct((2, ROWS, WIDE), F32),
        in_specs=[vmem] * 5,
        out_specs=anywhere,
        scratch_shapes=[pltpu.VMEM((2, ROWS, 2 * LANES), F32), sem((8,))],
        compiler_params=pltpu.CompilerParams(vmem_limit_bytes=16 << 20),
    )(*done)


def solution(mesh):
    placed = (P("row", "col"), P("row"), P(None, "col"), P("col"), P("col"))
    return jax.shard_map(
        on_device, mesh=mesh, in_specs=placed, out_specs=P(None, "row", "col"), check_vma=False
    )
```
